32 devices in a mesh: grp: 4 (over y, x), side: 2 (over core), seq: 4 (over z).
Axes of the slice: x: 2, y: 2, z: 4, core: 2. Of those that a mesh axis runs over, the one named last changes fastest.
Arguments:
- queries: bfloat16 [2, 4, 256, 64, 576], P('side', 'grp', 'seq'), may hold values from -48 to 48
- stream_rows: bfloat16 [2, 4, 256, 576], P('side', 'grp', 'seq'), may hold values from -6 to 6
- span_latents: bfloat16 [4, 256, 576], P('grp', 'seq'), may hold values from -6 to 6
- decode_cache: bfloat16 [65536, 576], P(('grp', 'seq')), may hold values from -6 to 6
- cache_lengths: int32 [16, 64], P(('grp', 'seq')), may hold values from 1 to 256, 4096 in all within a row
- block_owner: int32 [32, 1], replicated, may hold values from 0 to 15; in each aligned block of 32 rows (0 to 31, 32 to 63, ...) at most 4 rows name the same one
- block_request: int32 [32], replicated, may hold values from 0 to 63
Outputs:
- attended: bfloat16 [2, 4, 256, 64, 512], P('side', 'grp', 'seq')
The draws below stay inside these ranges and needn't reach their ends.
Inputs may be any that keep to these rules, and one draw needn't show every extreme that they name: Each row of cache_lengths sums to 4096; a device's requests take consecutive rows of its 4096 resident rows in order. `block_owner`: decode devices are numbered grp index * 4 + seq index; no device receives more than 4 blocks.
All inputs are finite; a program needn't handle non-finite values.
Results may differ from the reference program's by a relative error of at most 0.0048.
Values may be sent and summed in bfloat16 or wider, within the bound.
No kernel may reach another device: no remote copies, remote signals or barrier semaphores. Data moves between devices by JAX's collectives and lax.ppermute only.
A program may use at most 128 MiB of HBM per device.

```python
import math
import jax
import jax.numpy as jnp
import numpy as np
from jax import lax

HEADS = 64
LAT = 512
ROPE = 64
NOPE = 128
QROWS = 64
BLOCK = 32
CTX = 64
WIDE = 576
SPAN = 256
MAXIN = 4
POOL = 4096
MOSTLEN = 256
OWNERS = 16
BLOCKS = 32
N_GRP = 4
N_SEQ = 4


def draw_stream_rows(key, part):
    shape = (2, N_GRP, SPAN, LAT + ROPE)
    noise = jax.random.normal(jax.random.fold_in(key, 11), shape, jnp.float32)
    values = noise
    return jnp.clip(values, -6.0, 6.0).astype(jnp.bfloat16)


def draw_span_latents(key, part):
    shape = (N_GRP, SPAN, LAT + ROPE)
    noise = jax.random.normal(jax.random.fold_in(key, 12), shape, jnp.float32)
    values = noise
    return jnp.clip(values, -6.0, 6.0).astype(jnp.bfloat16)


def draw_decode_cache(key, part):
    shape = (N_GRP * N_SEQ * QROWS * CTX, LAT + ROPE)
    noise = jax.random.normal(jax.random.fold_in(key, 13), shape, jnp.float32)
    values = noise
    return jnp.clip(values, -6.0, 6.0).astype(jnp.bfloat16)


def draw_queries(key, part):
    shape = (2, N_GRP, SPAN, HEADS, LAT + ROPE)
    noise = jax.random.normal(jax.random.fold_in(key, 14), shape, jnp.float32)
    values = noise
    return jnp.clip(values, -48.0, 48.0).astype(jnp.bfloat16)


def with_ends(drawn, rng, least, high):
    spot = [jax.random.randint(jax.random.fold_in(rng, axis), (), 0, length) for axis, length in enumerate(drawn.shape)]
    longest = drawn.shape.index(max(drawn.shape))
    next_to = spot[:longest] + [(spot[longest] + 1) % drawn.shape[longest]] + spot[longest + 1:]
    return drawn.at[tuple(spot)].set(least).at[tuple(next_to)].set(high)


def length_profile(number_of, total, reach, lean):
    portions = [(1 << 20) // math.isqrt(grade ** lean) + 1 for grade in range(2, number_of + 1)]
    surplus, holding = total - reach - (number_of - 1), [1] * (number_of - 1)
    while surplus > 0:
        movable = [i for i in range(number_of - 1) if holding[i] < reach]
        pool, left = sum([portions[i] for i in movable]), surplus
        for i in movable:
            more = min(reach - holding[i], max(1, left * portions[i] // pool), surplus)
            holding[i] = holding[i] + more
            surplus = surplus - more
    return np.array([reach] + holding)


def ragged_sizes(own_key, number_of, total, limit, lean):
    if number_of == 2:
        one = jax.random.randint(own_key, (), max(1, total - limit), min(limit, total - 1) + 1)
        return jnp.stack([one, total - one])
    tallies = jnp.asarray(length_profile(number_of, total, limit, lean), jnp.int32)
    couples = (number_of - 1) // 2
    giver, sink = tallies[1:1 + 2 * couples:2], tallies[2:2 + 2 * couples:2]
    slack = jnp.minimum(giver - 1, limit - sink)
    moved = jax.random.randint(jax.random.fold_in(own_key, 1), (couples,), 0, 1 << 20) % (slack + 1)
    tallies = tallies.at[1:1 + 2 * couples:2].set(giver - moved).at[2:2 + 2 * couples:2].set(sink + moved)
    return tallies[jax.random.permutation(jax.random.fold_in(own_key, 2), number_of)]


def shared_out(stream_key, own, number, rows, amount, top, bound, lean):
    sequence = jax.random.permutation(stream_key, amount)
    crowded, usual = load_shares(amount, rows * top, bound, lean, True), load_shares(amount, rows * top, bound, lean, False)
    places = jnp.arange(amount)

    def named(tallies, turn):
        used = int((tallies > 0).sum())
        fixed = max(1, used // 4)
        passed = fixed + (places - fixed + turn * (used - fixed)) % max(1, amount - fixed)
        return jnp.zeros((amount,), jnp.int32).at[sequence[jnp.where(places < fixed, places, passed)]].set(jnp.asarray(tallies, jnp.int32))

    tallies = jnp.where(number % 4 == 0, named(crowded, number // 4), named(usual, number - number // 4 - 1))
    mixed = jax.random.permutation(jax.random.fold_in(own, 3), amount)
    donor, taker = mixed[0:amount // 2 * 2:2], mixed[1:amount // 2 * 2:2]
    room = jnp.minimum(tallies[donor] - 1, bound - tallies[taker]) // 2
    room = jnp.where((donor == sequence[0]) | (taker == sequence[0]) | (tallies[taker] == 0), 0, jnp.maximum(room, 0))
    passed = jax.random.randint(jax.random.fold_in(own, 4), (amount // 2,), 0, 1 << 20) % (room + 1)
    tallies = tallies.at[donor].add(-passed).at[taker].add(passed)
    items = jnp.searchsorted(jnp.cumsum(tallies), jnp.arange(rows * top), side="right").astype(jnp.int32)
    table = items.reshape(top, rows).T
    table = table[jax.random.permutation(jax.random.fold_in(own, 1), rows)]
    turn = jax.random.randint(jax.random.fold_in(own, 2), (rows, 1), 0, top)
    return jnp.take_along_axis(table, (jnp.arange(top)[None, :] + turn) % top, axis=1)


def load_shares(amount, total, reach, lean, full):
    portions = [(1 << 20) // math.isqrt(standing ** lean) + 1 for standing in range(1, amount + 1)]
    largest = reach if full else min(reach, max(-(-total // amount), total * portions[0] // sum(portions)))
    least = 1 if total - largest >= amount - 1 else 0
    given, rest = [largest] + [least] * (amount - 1), total - largest - least * (amount - 1)
    while rest > 0:
        free = [i for i in range(1, amount) if given[i] < largest] or [i for i in range(1, amount) if given[i] < reach]
        mass, budget = sum([portions[i] for i in free]), rest
        for i in free:
            addition = min(reach - given[i], max(1, budget * portions[i] // mass), rest)
            given[i] = given[i] + addition
            rest = rest - addition
    return np.array(given)


def setup_inputs(seed: int = 0) -> dict:
    key_list = jax.random.split(jax.random.key(seed), 8)
    queries = draw_queries(jax.random.fold_in(key_list[7], 71), 0)
    stream_rows = draw_stream_rows(jax.random.fold_in(key_list[7], 71), 0)
    span_latents = draw_span_latents(jax.random.fold_in(key_list[7], 71), 0)
    decode_cache = draw_decode_cache(jax.random.fold_in(key_list[7], 71), 0)
    cache_lengths = jax.vmap(lambda own: ragged_sizes(own, QROWS, POOL, MOSTLEN, 2))(jax.random.split(key_list[4], OWNERS)).reshape((OWNERS, QROWS)).astype(jnp.int32)
    block_owner_keys = jax.random.split(jax.random.fold_in(key_list[5], 1), BLOCKS // BLOCKS)
    block_owner_turns = jax.random.permutation(jax.random.fold_in(key_list[5], 3), BLOCKS // BLOCKS)
    block_owner = jax.vmap(lambda own, number: shared_out(jax.random.fold_in(key_list[5], 2), own, number, BLOCKS, OWNERS, 1, MAXIN, 2))(block_owner_keys, block_owner_turns).reshape((BLOCKS, 1))
    block_request = with_ends(jax.random.randint(key_list[6], (BLOCKS,), 0, QROWS), jax.random.fold_in(key_list[6], 1), 0, QROWS - 1).astype(jnp.int32)
    return {"queries": queries, "stream_rows": stream_rows, "span_latents": span_latents, "decode_cache": decode_cache, "cache_lengths": cache_lengths, "block_owner": block_owner, "block_request": block_request}


def masked_weights(score_rows, allowed):
    masked = jnp.where(allowed, score_rows, -jnp.inf)
    largest = lax.optimization_barrier(jnp.max(masked, axis=-1, keepdims=True))
    lifted = jnp.exp(masked - largest)
    return (lifted / lax.optimization_barrier(jnp.sum(lifted, axis=-1, keepdims=True))).astype(jnp.bfloat16)

def prefill_group(group_query, key_rows):
    factor = 1.0 / math.sqrt(NOPE + ROPE)
    allowed = (jnp.arange(2 * SPAN) - SPAN)[None, :] <= jnp.arange(SPAN)[:, None]
    key_wide = key_rows.astype(jnp.float32)

    def one_head(head_query):
        scored = jnp.einsum('qw,kw->qk', head_query.astype(jnp.float32), key_wide, precision=lax.Precision.HIGHEST) * factor
        weights = masked_weights(scored, allowed)
        return jnp.einsum('qk,kl->ql', weights.astype(jnp.float32), key_wide[:, :LAT], precision=lax.Precision.HIGHEST).astype(jnp.bfloat16)
    per_head = lax.map(one_head, jnp.transpose(group_query, (1, 0, 2)))
    return jnp.transpose(per_head, (1, 0, 2))

def reference(queries, stream_rows, span_latents, decode_cache, cache_lengths, block_owner, block_request):
    factor = 1.0 / math.sqrt(NOPE + ROPE)
    prefill = jnp.stack([prefill_group(queries[0, grp_number], jnp.concatenate([stream_rows[0, grp_number], span_latents[grp_number]], 0)) for grp_number in range(N_GRP)])
    owners = block_owner[:, 0]
    blocks_all = stream_rows[0].reshape(BLOCKS, BLOCK, WIDE)
    block_ids = jnp.arange(BLOCKS, dtype=jnp.int32)

    def one_owner(inputs):
        owner, owner_query, own_latent, pool_rows, lengths = inputs
        order_key = jnp.where(owners == owner, block_ids, BLOCKS + block_ids)
        picked = jnp.argsort(order_key)[:MAXIN]
        present = owners[picked] == owner
        requests = block_request[picked]
        arrived = blocks_all[picked].reshape(MAXIN * BLOCK, WIDE).astype(jnp.float32)
        arrived_allowed = jnp.repeat(present[None, :] & (requests[None, :] == jnp.arange(QROWS)[:, None]), BLOCK, axis=1)
        offsets = (jnp.cumsum(lengths) - lengths).astype(jnp.int32)
        padded = jnp.concatenate([pool_rows.astype(jnp.float32), jnp.zeros((MOSTLEN, WIDE), jnp.float32)], 0)
        windows = jax.vmap(lambda offset: lax.dynamic_slice_in_dim(padded, offset, MOSTLEN, 0))(offsets)
        query_wide = owner_query.astype(jnp.float32)
        latent_wide = own_latent.astype(jnp.float32)
        resident = jnp.einsum('rhw,rtw->rht', query_wide, windows, precision=lax.Precision.HIGHEST)
        incoming = jnp.einsum('rhw,kw->rhk', query_wide, arrived, precision=lax.Precision.HIGHEST)
        itself = jnp.einsum('rhw,rw->rh', query_wide, latent_wide, precision=lax.Precision.HIGHEST)[:, :, None]
        scored = jnp.concatenate([resident, incoming, itself], -1) * factor
        resident_allowed = jnp.arange(MOSTLEN)[None, :] < lengths[:, None]
        allowed = jnp.concatenate([resident_allowed, arrived_allowed, jnp.ones((QROWS, 1), jnp.bool_)], -1)[:, None, :]
        weights = masked_weights(scored, allowed).astype(jnp.float32)
        context = jnp.einsum('rht,rtl->rhl', weights[:, :, :MOSTLEN], windows[:, :, :LAT], precision=lax.Precision.HIGHEST)
        context = context + jnp.einsum('rhk,kl->rhl', weights[:, :, MOSTLEN:MOSTLEN + MAXIN * BLOCK], arrived[:, :LAT], precision=lax.Precision.HIGHEST)
        context = context + weights[:, :, MOSTLEN + MAXIN * BLOCK:] * latent_wide[:, None, :LAT]
        return context.astype(jnp.bfloat16)
    decoded = lax.map(one_owner, (jnp.arange(OWNERS, dtype=jnp.int32), queries[1].reshape(OWNERS, QROWS, HEADS, WIDE), stream_rows[1].reshape(OWNERS, QROWS, WIDE), decode_cache.reshape(OWNERS, POOL, WIDE), cache_lengths))
    return jnp.stack([prefill, decoded.reshape(N_GRP, SPAN, HEADS, LAT)])
```

```python
import functools
import math

import jax
import jax.numpy as jnp
from jax import lax
from jax.experimental import pallas as pl
from jax.experimental.pallas import tpu as pltpu
from jax.sharding import PartitionSpec as P

LAT = 512
ROPE = 64
NOPE = 128
BLOCK = 32
MAXIN = 4
ROWS = 256
TILE = 256
SCALE2 = math.log2(math.e) / math.sqrt(NOPE + ROPE)


NT = (((1,), (1,)), ((), ()))
ANY = pl.BlockSpec(memory_space=pl.ANY)
VMEM = pl.BlockSpec(memory_space=pltpu.VMEM)
SMEM = pl.BlockSpec(memory_space=pltpu.SMEM)


def slot_tables(owner_ref, request_ref, me, slot_block, slot_request, slot_count):
    slot_count[0] = 0
    for j in range(MAXIN):
        slot_block[j] = 0
        slot_request[j] = -1

    @pl.loop(0, owner_ref.shape[1])
    def _(b):
        @pl.when(owner_ref[0, b] == me)
        def _():
            j = slot_count[0]
            slot_block[j] = b
            slot_request[j] = request_ref[b]
            slot_count[0] = j + 1


def pick_kernel(place_ref, owner_ref, *refs, n_seq, n_grp):
    chunks, outs, counts, ranks = refs[:n_seq], refs[n_seq:-2], refs[-2], refs[-1]
    side, grp, seq = place_ref[0], place_ref[1], place_ref[2]
    per_device = chunks[0].shape[0] // 2 // BLOCK

    @pl.when(side == 0)
    def _():
        @pl.loop(0, n_grp * n_seq)
        def _(o):
            counts[o] = 0

        @pl.loop(0, owner_ref.shape[1])
        def _(b):
            o = owner_ref[0, b]
            ranks[b] = counts[o]
            counts[o] = counts[o] + 1

        for far in range(n_seq):
            for half in range(per_device):
                b = (grp * n_seq + (seq ^ far)) * per_device + half
                owner = owner_ref[0, b]
                apart = (owner // n_seq) ^ grp
                at = pl.multiple_of(ranks[b] * BLOCK, BLOCK)
                for d in range(n_grp):

                    @pl.when((owner % n_seq == seq) & (apart == d))
                    def _(far=far, half=half, at=at, d=d):
                        outs[d][pl.ds(at, BLOCK), :] = chunks[far][half * BLOCK : (half + 1) * BLOCK, :]


def main_kernel(
    place_ref, lengths_ref, owner_ref, request_ref, q_hbm, own_ref, cache_hbm, *refs, n_seq
):
    chunks = refs[:n_seq]
    out_hbm, kept_acc, kept_max, kept_sum = refs[n_seq : n_seq + 4]
    (qbuf, kbuf, cbuf, obuf, acc, offsets, slot_block, slot_request, slot_count, qsem, csem, osem) = (
        refs[n_seq + 4 :]
    )
    side, grp, seq = place_ref[0], place_ref[1], place_ref[2]
    steps = q_hbm.shape[0] // ROWS
    tiles = cache_hbm.shape[1] // TILE
    requests = lengths_ref.shape[1]
    heads = q_hbm.shape[0] // requests
    per_step = ROWS // heads

    def q_copy(t):
        at = pl.multiple_of(t * ROWS, ROWS)
        return pltpu.make_async_copy(q_hbm.at[pl.ds(at, ROWS), :], qbuf.at[t], qsem.at[t])

    def c_copy(t):
        at = pl.multiple_of(t * TILE, TILE)
        return pltpu.make_async_copy(cache_hbm.at[:, pl.ds(at, TILE)], cbuf.at[t], csem.at[t])

    def o_copy(t):
        at = pl.multiple_of(t * ROWS, ROWS)
        return pltpu.make_async_copy(
            obuf.at[t % 2], out_hbm.at[pl.ds(at, ROWS), :], osem.at[t % 2]
        )

    def put(t, value):
        @pl.when(t >= 2)
        def _():
            o_copy(t - 2).wait()

        obuf[t % 2] = value
        o_copy(t).start()

    row = lax.broadcasted_iota(jnp.int32, (ROWS, 1), 0) // heads

    @pl.when(side == 0)
    def _():
        @pl.loop(0, steps)
        def _(t):
            q_copy(t).start()

        width = chunks[0].shape[0]
        for far in range(n_seq):
            kbuf[far * width : (far + 1) * width, :] = chunks[far][...]
        keys = n_seq * width
        col = lax.broadcasted_iota(jnp.int32, (1, keys), 1)
        inner = col % width
        source = seq ^ (col // width)
        least = jnp.where(inner < width // 2, -1, inner - width // 2 - (seq - source) * (width // 2))

        @pl.loop(0, steps)
        def _(t):
            q_copy(t).wait()
            scores = lax.dot_general(qbuf[t], kbuf[...], NT, preferred_element_type=jnp.float32)
            scores = jnp.where(least <= row + t * per_step, scores, -jnp.inf)
            top = jnp.max(scores, axis=1, keepdims=True)
            lifted = jnp.exp2((scores - top) * SCALE2)
            total = jnp.sum(lifted, axis=1, keepdims=True)
            mixed = jnp.dot(
                lifted.astype(jnp.bfloat16), kbuf[:, :LAT], preferred_element_type=jnp.float32
            )
            put(t, (mixed * (1.0 / total)).astype(jnp.bfloat16))

    @pl.when(side == 1)
    def _():
        @pl.loop(0, steps)
        def _(t):
            q_copy(t).start()
            c_copy(t).start()

        offsets[0] = 0

        @pl.loop(0, requests)
        def _(r):
            offsets[r + 1] = offsets[r] + lengths_ref[0, r]

        slot_tables(owner_ref, request_ref, grp * n_seq + seq, slot_block, slot_request, slot_count)

        def spread(first, table):
            value = table[first + per_step - 1]
            for k in range(per_step - 2, -1, -1):
                value = jnp.where(row == k, table[first + k], value)
            return value

        def one_step(t, ready):
            first = t * per_step
            q_copy(t).wait()
            q = qbuf[t]
            mine = lax.broadcasted_iota(jnp.int32, (ROWS, requests), 1) == row + first
            itself = lax.dot_general(q, own_ref[...], NT, preferred_element_type=jnp.float32)
            top = jnp.sum(jnp.where(mine, itself, 0.0), axis=1, keepdims=True)
            acc[...] = jnp.dot(
                mine.astype(jnp.bfloat16), own_ref[:, :LAT], preferred_element_type=jnp.float32
            )
            starts = spread(first, offsets)
            ends = spread(first + 1, offsets)

            def one_tile(k, carry):
                top, total, ready = carry

                @pl.when(k >= ready)
                def _():
                    c_copy(k).wait()

                place = lax.broadcasted_iota(jnp.int32, (1, TILE), 1) + k * TILE
                scores = jnp.dot(q, cbuf[k], preferred_element_type=jnp.float32)
                scores = jnp.where((place >= starts) & (place < ends), scores, -jnp.inf)
                higher = jnp.maximum(top, jnp.max(scores, axis=1, keepdims=True))
                lifted = jnp.exp2((scores - higher) * SCALE2)
                fade = jnp.exp2((top - higher) * SCALE2)
                total = total * fade + jnp.sum(lifted, axis=1, keepdims=True)
                acc[...] = acc[...] * fade + lax.dot_general(
                    lifted.astype(jnp.bfloat16),
                    cbuf[k, :LAT, :],
                    NT,
                    preferred_element_type=jnp.float32,
                )
                return higher, total, jnp.maximum(ready, k + 1)

            top, total, ready = lax.fori_loop(
                offsets[first] // TILE,
                (offsets[first + per_step] + TILE - 1) // TILE,
                one_tile,
                (top, jnp.ones((ROWS, 1), jnp.float32), ready),
            )
            put(t, (acc[...] * (1.0 / total)).astype(jnp.bfloat16))
            for j in range(MAXIN):
                r = slot_request[j]
                for k in range(per_step):

                    @pl.when(r == first + k)
                    def _(j=j, k=k):
                        rows = slice(k * heads, (k + 1) * heads)
                        to = slice(j * heads, (j + 1) * heads)
                        kept_acc[to, :] = acc[rows, :]
                        kept_max[to, :] = jnp.broadcast_to(top[rows], (heads, 128))
                        kept_sum[to, :] = jnp.broadcast_to(total[rows], (heads, 128))

            return ready

        lax.fori_loop(0, steps, one_step, 0)

    o_copy(steps - 2).wait()
    o_copy(steps - 1).wait()


def merge_kernel(
    place_ref, owner_ref, request_ref, q_hbm, kept_acc, kept_max, kept_sum, *refs, n_grp, n_seq
):
    landed, out_hbm = refs[:n_grp], refs[n_grp + 1]
    (qbuf, arrived, obuf, slot_block, slot_request, slot_count, qsem, osem) = refs[n_grp + 2 :]
    side, grp, seq = place_ref[0], place_ref[1], place_ref[2]
    heads = qbuf.shape[0] // MAXIN
    per_group = owner_ref.shape[1] // n_grp

    @pl.when(side == 1)
    def _():
        slot_tables(owner_ref, request_ref, grp * n_seq + seq, slot_block, slot_request, slot_count)
        arrived[...] = jnp.zeros_like(arrived)

        def q_copy(j):
            at = pl.multiple_of(jnp.maximum(slot_request[j], 0) * heads, heads)
            return pltpu.make_async_copy(
                q_hbm.at[pl.ds(at, heads), :],
                qbuf.at[j * heads : (j + 1) * heads, :],
                qsem.at[j],
            )

        def o_copy(j):
            at = pl.multiple_of(jnp.maximum(slot_request[j], 0) * heads, heads)
            return pltpu.make_async_copy(
                obuf.at[j * heads : (j + 1) * heads, :],
                out_hbm.at[pl.ds(at, heads), :],
                osem.at[j],
            )

        def written(j):
            wanted = j < slot_count[0]
            for k in range(j):
                wanted = wanted & (slot_request[k] != slot_request[j])
            return wanted

        for j in range(MAXIN):
            q_copy(j).start()
        for j in range(MAXIN):
            apart = (slot_block[j] // per_group) ^ grp
            for d in range(n_grp):

                @pl.when((j < slot_count[0]) & (apart == d))
                def _(j=j, d=d):
                    rows = slice(j * BLOCK, (j + 1) * BLOCK)
                    arrived[rows, :] = landed[d][rows, :]

        def spread(index, size):
            value = slot_request[MAXIN - 1]
            for j in range(MAXIN - 2, -1, -1):
                value = jnp.where(index < (j + 1) * size, slot_request[j], value)
            return value

        query = lax.broadcasted_iota(jnp.int32, (MAXIN * heads, 1), 0)
        key = lax.broadcasted_iota(jnp.int32, (1, MAXIN * BLOCK), 1)
        allowed = (spread(query, heads) == spread(key, BLOCK)) & (key < slot_count[0] * BLOCK)
        for j in range(MAXIN):
            q_copy(j).wait()
        scores = lax.dot_general(qbuf[...], arrived[...], NT, preferred_element_type=jnp.float32)
        live = query < slot_count[0] * heads
        top = jnp.where(live, kept_max[:, :1], 0.0)
        scores = jnp.where(allowed, scores, -jnp.inf)
        higher = jnp.maximum(top, jnp.max(scores, axis=1, keepdims=True))
        lifted = jnp.exp2((scores - higher) * SCALE2)
        fade = jnp.exp2((top - higher) * SCALE2)
        total = kept_sum[:, :1] * fade + jnp.sum(lifted, axis=1, keepdims=True)
        mixed = kept_acc[...] * fade + jnp.dot(
            lifted.astype(jnp.bfloat16), arrived[:, :LAT], preferred_element_type=jnp.float32
        )
        obuf[...] = (mixed * (1.0 / total)).astype(jnp.bfloat16)
        for j in range(MAXIN):

            @pl.when(written(j))
            def _(j=j):
                o_copy(j).start()

        for j in range(MAXIN):

            @pl.when(written(j))
            def _(j=j):
                o_copy(j).wait()


def local(
    queries, stream_rows, span_latents, decode_cache, cache_lengths, block_owner, block_request
):
    n_grp, n_side, n_seq = (lax.axis_size(a) for a in ("grp", "side", "seq"))
    names = ("grp", "side", "seq")
    place = jnp.stack([lax.axis_index("side"), lax.axis_index("grp"), lax.axis_index("seq")])
    place = place.astype(jnp.int32)
    own_query, own_stream, own_span = queries[0, 0], stream_rows[0, 0], span_latents[0]
    rows, heads, width = own_query.shape
    q = own_query.reshape(rows * heads, width)
    cache = decode_cache.T
    owner = block_owner.T
    blocks = owner.shape[1]

    def at(grp, side, seq):
        return (grp * n_side + side) * n_seq + seq

    def along_seq(far):
        return [
            (at(g, 0, s), at(g, 0, s ^ far)) for g in range(n_grp) for s in range(n_seq)
        ]

    def across(apart):
        return [
            (at(g, 0, s), at(g ^ apart, 1, s)) for g in range(n_grp) for s in range(n_seq)
        ]

    chunk = jnp.concatenate([own_stream, own_span], 0)
    chunks = [chunk] + [lax.ppermute(chunk, names, along_seq(far)) for far in range(1, n_seq)]

    picked = pl.pallas_call(
        functools.partial(pick_kernel, n_seq=n_seq, n_grp=n_grp),
        out_shape=[jax.ShapeDtypeStruct((MAXIN * BLOCK, width), jnp.bfloat16)] * n_grp,
        in_specs=[SMEM, SMEM] + [VMEM] * n_seq,
        out_specs=[VMEM] * n_grp,
        scratch_shapes=[pltpu.SMEM((n_grp * n_seq,), jnp.int32), pltpu.SMEM((blocks,), jnp.int32)],
        name="pick",
    )(place, owner, *chunks)
    landed = [lax.ppermute(picked[d], names, across(d)) for d in range(n_grp)]

    steps = rows * heads // ROWS
    tiles = cache.shape[1] // TILE
    stats = jax.ShapeDtypeStruct((MAXIN * heads, 128), jnp.float32)
    out, kept_acc, kept_max, kept_sum = pl.pallas_call(
        functools.partial(main_kernel, n_seq=n_seq),
        out_shape=[
            jax.ShapeDtypeStruct((rows * heads, LAT), jnp.bfloat16),
            jax.ShapeDtypeStruct((MAXIN * heads, LAT), jnp.float32),
            stats,
            stats,
        ],
        in_specs=[SMEM] * 4 + [ANY, VMEM, ANY] + [VMEM] * n_seq,
        out_specs=[ANY, VMEM, VMEM, VMEM],
        scratch_shapes=[
            pltpu.VMEM((steps, ROWS, width), jnp.bfloat16),
            pltpu.VMEM((n_seq * 2 * rows, width), jnp.bfloat16),
            pltpu.VMEM((tiles, width, TILE), jnp.bfloat16),
            pltpu.VMEM((2, ROWS, LAT), jnp.bfloat16),
            pltpu.VMEM((ROWS, LAT), jnp.float32),
            pltpu.SMEM((rows + 1,), jnp.int32),
            pltpu.SMEM((MAXIN,), jnp.int32),
            pltpu.SMEM((MAXIN,), jnp.int32),
            pltpu.SMEM((1,), jnp.int32),
            pltpu.SemaphoreType.DMA((steps,)),
            pltpu.SemaphoreType.DMA((tiles,)),
            pltpu.SemaphoreType.DMA((2,)),
        ],
        cost_estimate=pl.CostEstimate(
            flops=2 * rows * heads * n_seq * 2 * rows * (width + LAT),
            bytes_accessed=2 * (q.size + cache.size + rows * heads * LAT),
            transcendentals=rows * heads * n_seq * 2 * rows,
        ),
        name="main",
    )(place, cache_lengths, owner, block_request, q, own_stream, cache, *chunks)

    out = pl.pallas_call(
        functools.partial(merge_kernel, n_grp=n_grp, n_seq=n_seq),
        out_shape=jax.ShapeDtypeStruct((rows * heads, LAT), jnp.bfloat16),
        in_specs=[SMEM] * 3 + [ANY] + [VMEM] * (3 + n_grp) + [ANY],
        out_specs=ANY,
        input_output_aliases={7 + n_grp: 0},
        scratch_shapes=[
            pltpu.VMEM((MAXIN * heads, width), jnp.bfloat16),
            pltpu.VMEM((MAXIN * BLOCK, width), jnp.bfloat16),
            pltpu.VMEM((MAXIN * heads, LAT), jnp.bfloat16),
            pltpu.SMEM((MAXIN,), jnp.int32),
            pltpu.SMEM((MAXIN,), jnp.int32),
            pltpu.SMEM((1,), jnp.int32),
            pltpu.SemaphoreType.DMA((MAXIN,)),
            pltpu.SemaphoreType.DMA((MAXIN,)),
        ],
        name="merge",
    )(place, owner, block_request, q, kept_acc, kept_max, kept_sum, *landed, out)
    return out.reshape(1, 1, rows, heads, LAT)


def solution(mesh):
    return jax.shard_map(
        local,
        mesh=mesh,
        in_specs=(
            P("side", "grp", "seq", None, None),
            P("side", "grp", "seq", None),
            P("grp", "seq", None),
            P(("grp", "seq"), None),
            P(("grp", "seq"), None),
            P(),
            P(),
        ),
        out_specs=P("side", "grp", "seq", None, None),
        check_vma=False,
    )
```

```python
import functools
import math

import jax
import jax.numpy as jnp
from jax import lax
from jax.experimental import pallas as pl
from jax.experimental.pallas import tpu as pltpu
from jax.sharding import PartitionSpec as P

LAT = 512
ROPE = 64
NOPE = 128
BLOCK = 32
MAXIN = 4
MOSTLEN = 256
SCORES = 2**19
TILE = 256
LANE = 128
AT_ONCE = 4
SCALE2 = math.log2(math.e) / math.sqrt(NOPE + ROPE)


NT = (((1,), (1,)), ((), ()))
ANY = pl.BlockSpec(memory_space=pl.ANY)
VMEM = pl.BlockSpec(memory_space=pltpu.VMEM)
SMEM = pl.BlockSpec(memory_space=pltpu.SMEM)


GRANT = 40 * 2**20


def fast(x):
    return pltpu.with_memory_space_constraint(x, pltpu.VMEM)


def slow(x):
    return pltpu.with_memory_space_constraint(x, pltpu.HBM)


def fast_shape(shape, dtype):
    return pltpu.VMEM(shape, dtype)


PLACE = 3


def fetch_kernel(info_ref, q_hbm, table, q_out, counts, sem, *, blocks, n_grp, n_seq):
    copy = pltpu.make_async_copy(q_hbm, q_out, sem)
    copy.start()
    known = info_ref.shape[0]
    me = info_ref[1] * n_seq + info_ref[2]

    @pl.loop(0, known)
    def _(i):
        table[i] = info_ref[i]

    @pl.loop(0, n_grp * n_seq)
    def _(o):
        counts[o] = 0

    for j in range(MAXIN):
        table[known + blocks + 1 + j] = 0
        table[known + blocks + 1 + MAXIN + j] = -1

    @pl.loop(0, blocks)
    def _(b):
        owner = info_ref[PLACE + b]
        rank = counts[owner]
        table[known + b] = rank
        counts[owner] = rank + 1

        @pl.when(owner == me)
        def _():
            table[known + blocks + 1 + rank] = b
            table[known + blocks + 1 + MAXIN + rank] = info_ref[PLACE + blocks + b]

    table[known + blocks] = counts[me]
    copy.wait()


class Slots:
    def __init__(self, table, blocks):
        self.table, self.at = table, table.shape[0] - 2 * MAXIN - 1

    def count(self):
        return self.table[self.at]

    def block(self, j):
        return self.table[self.at + 1 + j]

    def request(self, j):
        return self.table[self.at + 1 + MAXIN + j]


def pick_kernel(table, *refs, n_seq, n_grp, blocks):
    chunks, outs = refs[:n_seq], refs[n_seq:]
    side, grp, seq = table[0], table[1], table[2]
    ranks = table.shape[0] - 2 * MAXIN - 1 - blocks
    per_device = chunks[0].shape[0] // 2 // BLOCK

    @pl.when(side == 0)
    def _():
        for far in range(n_seq):
            for half in range(per_device):
                b = (grp * n_seq + (seq ^ far)) * per_device + half
                owner = table[PLACE + b]
                apart = (owner // n_seq) ^ grp
                at = pl.multiple_of(table[ranks + b] * BLOCK, BLOCK)

                @pl.when(owner % n_seq == seq)
                def _(far=far, half=half, at=at, apart=apart):
                    for d in range(n_grp):

                        @pl.when(apart == d)
                        def _(d=d):
                            outs[d][pl.ds(at, BLOCK), :] = chunks[far][
                                half * BLOCK : (half + 1) * BLOCK, :
                            ]


def main_kernel(table, q_ref, cache_hbm, *refs, n_seq, blocks, step):
    chunks = refs[:n_seq]
    out_hbm, kept_acc, kept_max, kept_sum = refs[n_seq : n_seq + 4]
    (kbuf, cbuf, obuf, dbuf, scores_ref, best, sums, acc, own32, offsets, csem, osem) = refs[
        n_seq + 4 :
    ]
    side, seq = table[0], table[2]
    requests = chunks[0].shape[0] // 2
    heads = q_ref.shape[0] // requests
    steps = q_ref.shape[0] // step
    per_step = step // heads

    def o_copy(t):
        return pltpu.make_async_copy(
            obuf.at[t % 2], out_hbm.at[t * step : (t + 1) * step, :], osem.at[t % 2]
        )

    @pl.when(side == 0)
    def _():
        half = chunks[0].shape[0] // 2
        keys = n_seq * half
        for far in range(n_seq):
            kbuf[far * half : (far + 1) * half, :] = chunks[far][:half, :]
            kbuf[keys + far * half : keys + (far + 1) * half, :] = chunks[far][half:, :]
        col = lax.broadcasted_iota(jnp.int32, (1, keys), 1)
        source = seq ^ (col // half)
        least = col % half + (source - seq) * half

        def score(t):
            scores_ref[...] = lax.dot_general(
                q_ref[t * step : (t + 1) * step, :],
                kbuf[...],
                NT,
                preferred_element_type=jnp.float32,
            )

        def finish(t):
            scores = scores_ref[...]
            late = []
            for k in range(per_step):
                hidden = jnp.where(least <= t * per_step + k, 0.0, -jnp.inf)
                late.append(scores[k * heads : (k + 1) * heads, keys:] + hidden)
            late = jnp.concatenate(late, 0)
            early = scores[:, :keys]
            top = jnp.maximum(
                jnp.max(early, axis=1, keepdims=True), jnp.max(late, axis=1, keepdims=True)
            )
            shift = top * SCALE2
            early = jnp.exp2(early * SCALE2 - shift)
            late = jnp.exp2(late * SCALE2 - shift)
            total = jnp.sum(early, axis=1, keepdims=True) + jnp.sum(late, axis=1, keepdims=True)
            lifted = jnp.concatenate([early.astype(jnp.bfloat16), late.astype(jnp.bfloat16)], 1)
            mixed = jnp.dot(lifted, kbuf[:, :LAT], preferred_element_type=jnp.float32)
            if t >= 2:
                o_copy(t - 2).wait()
            obuf[t % 2] = (mixed * (1.0 / total)).astype(jnp.bfloat16)
            o_copy(t).start()

        for t in range(steps):
            score(t)
            finish(t)
        o_copy(steps - 2).wait()
        o_copy(steps - 1).wait()

    @pl.when(side == 1)
    def _():
        chunks_in = cache_hbm.shape[1] // TILE
        lanes = cache_hbm.shape[1] // LANE
        size = AT_ONCE * heads
        bodies = requests // AT_ONCE

        def c_copy(k):
            at = pl.multiple_of(k * TILE, TILE)
            return pltpu.make_async_copy(
                cache_hbm.at[:, pl.ds(at, TILE)], cbuf.at[:, pl.ds(at, TILE)], csem.at[k]
            )

        def d_copy(t):
            at = pl.multiple_of(t * size, size)
            return pltpu.make_async_copy(
                dbuf.at[t % 2], out_hbm.at[pl.ds(at, size), :], osem.at[t % 2]
            )

        @pl.loop(0, chunks_in)
        def _(k):
            c_copy(k).start()

        own32[...] = chunks[0][:requests, :].astype(jnp.float32)
        offsets[0] = 0

        @pl.loop(0, requests)
        def _(r):
            offsets[r + 1] = offsets[r] + table[PLACE + 2 * blocks + r]

        slots = Slots(table, blocks)

        def body(t, count):
            span = count * LANE
            lane = lax.broadcasted_iota(jnp.int32, (1, span), 1)
            each = range(AT_ONCE)
            at = [pl.multiple_of((t * AT_ONCE + u) * heads, heads) for u in each]
            low = [offsets[t * AT_ONCE + u] for u in range(AT_ONCE + 1)]
            start = [
                pl.multiple_of(jnp.minimum(low[u] // LANE, lanes - count) * LANE, LANE)
                for u in each
            ]
            q = q_ref[pl.ds(pl.multiple_of(at[0], size), size), :]
            q = [q[u * heads : (u + 1) * heads] for u in each]
            own = [own32[pl.ds(t * AT_ONCE + u, 1), :] for u in each]
            scores = [
                jnp.dot(q[u], cbuf[:, pl.ds(start[u], span)], preferred_element_type=jnp.float32)
                for u in each
            ]
            itself = [
                jnp.sum(q[u].astype(jnp.float32) * own[u], axis=1, keepdims=True) for u in each
            ]
            for u in each:
                place = lane + start[u]
                hidden = jnp.where((place >= low[u]) & (place < low[u + 1]), 0.0, -jnp.inf)
                scores[u] = scores[u] + hidden
            top = [
                jnp.maximum(jnp.max(scores[u], axis=1, keepdims=True), itself[u]) for u in each
            ]
            lifted = [jnp.exp2(scores[u] * SCALE2 - top[u] * SCALE2) for u in each]
            lead = [jnp.exp2((itself[u] - top[u]) * SCALE2) for u in each]
            mixed = [
                lax.dot_general(
                    lifted[u].astype(jnp.bfloat16),
                    cbuf[:LAT, pl.ds(start[u], span)],
                    NT,
                    preferred_element_type=jnp.float32,
                )
                for u in each
            ]
            total = [lead[u] + jnp.sum(lifted[u], axis=1, keepdims=True) for u in each]
            mixed = [mixed[u] + lead[u] * own[u][:, :LAT] for u in each]
            scaled = [(mixed[u] * (1.0 / total[u])).astype(jnp.bfloat16) for u in each]
            whole = pl.ds(at[0], size)
            dbuf[t % 2] = jnp.concatenate(scaled, 0)
            acc[whole, :] = jnp.concatenate(mixed, 0)
            best[whole, :] = jnp.broadcast_to(jnp.concatenate(top, 0), (size, LANE))
            sums[whole, :] = jnp.broadcast_to(jnp.concatenate(total, 0), (size, LANE))

        def one_body(t, ready):
            first = t * AT_ONCE

            count = 1
            for u in range(AT_ONCE):
                low, high = offsets[first + u], offsets[first + u + 1]
                count = jnp.maximum(count, (high + LANE - 1) // LANE - low // LANE)
            end = jnp.minimum(offsets[first + AT_ONCE - 1] // LANE, lanes - count) + count
            need = (end * LANE + TILE - 1) // TILE

            @pl.loop(ready, need)
            def _(k):
                c_copy(k).wait()

            @pl.when(t >= 2)
            def _():
                d_copy(t - 2).wait()

            for c in range(1, MOSTLEN // LANE + 2):

                @pl.when(count == c)
                def _(c=c):
                    body(t, c)

            d_copy(t).start()
            return jnp.maximum(ready, need)

        ready = lax.fori_loop(0, bodies, one_body, 0)

        @pl.loop(ready, chunks_in)
        def _(k):
            c_copy(k).wait()

        for j in range(MAXIN):
            at = pl.multiple_of(jnp.maximum(slots.request(j), 0) * heads, heads)
            to = slice(j * heads, (j + 1) * heads)
            kept_acc[to, :] = acc[pl.ds(at, heads), :]
            kept_max[to, :] = best[pl.ds(at, heads), :]
            kept_sum[to, :] = sums[pl.ds(at, heads), :]
        d_copy(bodies - 2).wait()
        d_copy(bodies - 1).wait()


def merge_kernel(
    table,
    q_ref,
    kept_acc,
    kept_max,
    kept_sum,
    *refs,
    n_grp,
    n_seq,
    per_group,
):
    landed, out_hbm = refs[:n_grp], refs[n_grp + 1]
    qbuf, arrived, obuf, osem = refs[n_grp + 2 :]
    side, grp = table[0], table[1]
    heads = qbuf.shape[0] // MAXIN
    slots = Slots(table, per_group * n_grp)

    @pl.when((side == 1) & (slots.count() > 0))
    def _():
        arrived[...] = jnp.zeros_like(arrived)

        def o_copy(j):
            at = pl.multiple_of(jnp.maximum(slots.request(j), 0) * heads, heads)
            return pltpu.make_async_copy(
                obuf.at[j * heads : (j + 1) * heads, :],
                out_hbm.at[pl.ds(at, heads), :],
                osem.at[j],
            )

        def written(j):
            wanted = j < slots.count()
            for k in range(j):
                wanted = wanted & (slots.request(k) != slots.request(j))
            return wanted

        for j in range(MAXIN):
            at = pl.multiple_of(jnp.maximum(slots.request(j), 0) * heads, heads)
            qbuf[j * heads : (j + 1) * heads, :] = q_ref[pl.ds(at, heads), :]
            apart = (slots.block(j) // per_group) ^ grp
            for d in range(n_grp):

                @pl.when((j < slots.count()) & (apart == d))
                def _(j=j, d=d):
                    rows = slice(j * BLOCK, (j + 1) * BLOCK)
                    arrived[rows, :] = landed[d][rows, :]

        def spread(index, size):
            value = slots.request(MAXIN - 1)
            for j in range(MAXIN - 2, -1, -1):
                value = jnp.where(index < (j + 1) * size, slots.request(j), value)
            return value

        query = lax.broadcasted_iota(jnp.int32, (MAXIN * heads, 1), 0)
        key = lax.broadcasted_iota(jnp.int32, (1, MAXIN * BLOCK), 1)
        allowed = (spread(query, heads) == spread(key, BLOCK)) & (key < slots.count() * BLOCK)
        live = query < slots.count() * heads
        scores = lax.dot_general(qbuf[...], arrived[...], NT, preferred_element_type=jnp.float32)
        top = jnp.where(live, kept_max[:, :1], 0.0)
        scores = jnp.where(allowed, scores, -jnp.inf)
        higher = jnp.maximum(top, jnp.max(scores, axis=1, keepdims=True))
        shift = higher * SCALE2
        lifted = jnp.exp2(scores * SCALE2 - shift)
        fade = jnp.exp2(top * SCALE2 - shift)
        total = kept_sum[:, :1] * fade + jnp.sum(lifted, axis=1, keepdims=True)
        mixed = kept_acc[...] * fade + jnp.dot(
            lifted.astype(jnp.bfloat16), arrived[:, :LAT], preferred_element_type=jnp.float32
        )
        obuf[...] = (mixed * (1.0 / total)).astype(jnp.bfloat16)
        for j in range(MAXIN):

            @pl.when(written(j))
            def _(j=j):
                o_copy(j).start()

        for j in range(MAXIN):

            @pl.when(written(j))
            def _(j=j):
                o_copy(j).wait()


def local(
    queries, stream_rows, span_latents, decode_cache, cache_lengths, block_owner, block_request
):
    n_grp, n_side, n_seq = (lax.axis_size(a) for a in ("grp", "side", "seq"))
    names = ("grp", "side", "seq")
    place = [lax.axis_index(a).astype(jnp.int32).reshape(1) for a in ("side", "grp", "seq")]
    blocks = block_request.shape[0]
    info = jnp.concatenate([*place, block_owner[:, 0], block_request, cache_lengths[0]])
    own_query, own_stream, own_span = queries[0, 0], stream_rows[0, 0], span_latents[0]
    rows, heads, width = own_query.shape
    q = slow(own_query.reshape(rows * heads, width))
    size = info.shape[0] + blocks + 1 + 2 * MAXIN
    cache = slow(decode_cache.T)

    def at(grp, side, seq):
        return (grp * n_side + side) * n_seq + seq

    def along_seq(far):
        return [
            (at(g, 0, s), at(g, 0, s ^ far)) for g in range(n_grp) for s in range(n_seq)
        ]

    def across(apart):
        return [
            (at(g, 0, s), at(g ^ apart, 1, s)) for g in range(n_grp) for s in range(n_seq)
        ]

    chunk = jnp.concatenate([own_stream, own_span], 0)
    chunks = [chunk] + [lax.ppermute(chunk, names, along_seq(far)) for far in range(1, n_seq)]
    chunks = [fast(x) for x in chunks]

    table, q_fast = pl.pallas_call(
        functools.partial(fetch_kernel, blocks=blocks, n_grp=n_grp, n_seq=n_seq),
        out_shape=[jax.ShapeDtypeStruct((size,), jnp.int32), fast_shape(q.shape, q.dtype)],
        in_specs=[SMEM, ANY],
        out_specs=[SMEM, VMEM],
        scratch_shapes=[pltpu.SMEM((n_grp * n_seq,), jnp.int32), pltpu.SemaphoreType.DMA],
        compiler_params=pltpu.CompilerParams(vmem_limit_bytes=GRANT),
        cost_estimate=pl.CostEstimate(flops=0, bytes_accessed=4 * q.size, transcendentals=0),
        name="fetch",
    )(info, q)
    q_fast = fast(q_fast)

    picked = pl.pallas_call(
        functools.partial(pick_kernel, n_seq=n_seq, n_grp=n_grp, blocks=blocks),
        out_shape=[fast_shape((MAXIN * BLOCK, width), jnp.bfloat16)] * n_grp,
        in_specs=[SMEM] + [VMEM] * n_seq,
        out_specs=[VMEM] * n_grp,
        compiler_params=pltpu.CompilerParams(vmem_limit_bytes=GRANT),
        name="pick",
    )(table, *chunks)
    landed = [fast(lax.ppermute(picked[d], names, across(d))) for d in range(n_grp)]

    tiles = cache.shape[1] // TILE
    keys = n_seq * 2 * rows
    step = min(rows * heads, max(heads, SCORES // keys))
    stats = fast_shape((MAXIN * heads, 128), jnp.float32)
    out, *kept = pl.pallas_call(
        functools.partial(main_kernel, n_seq=n_seq, blocks=blocks, step=step),
        out_shape=[
            jax.ShapeDtypeStruct((rows * heads, LAT), jnp.bfloat16),
            fast_shape((MAXIN * heads, LAT), jnp.float32),
            stats,
            stats,
        ],
        in_specs=[SMEM, VMEM, ANY] + [VMEM] * n_seq,
        out_specs=[ANY] + [VMEM] * 3,
        scratch_shapes=[
            pltpu.VMEM((keys, width), jnp.bfloat16),
            pltpu.VMEM(cache.shape, jnp.bfloat16),
            pltpu.VMEM((2, step, LAT), jnp.bfloat16),
            pltpu.VMEM((2, AT_ONCE * heads, LAT), jnp.bfloat16),
            pltpu.VMEM((step, keys), jnp.float32),
            pltpu.VMEM((rows * heads, LANE), jnp.float32),
            pltpu.VMEM((rows * heads, LANE), jnp.float32),
            pltpu.VMEM((rows * heads, LAT), jnp.float32),
            pltpu.VMEM((rows, width), jnp.float32),
            pltpu.SMEM((rows + 1,), jnp.int32),
            pltpu.SemaphoreType.DMA((tiles,)),
            pltpu.SemaphoreType.DMA((2,)),
        ],
        compiler_params=pltpu.CompilerParams(vmem_limit_bytes=GRANT),
        cost_estimate=pl.CostEstimate(
            flops=2 * rows * heads * keys * (width + LAT),
            bytes_accessed=2 * (q.size + cache.size + rows * heads * LAT),
            transcendentals=rows * heads * keys,
        ),
        name="main",
    )(table, q_fast, cache, *chunks)

    out = pl.pallas_call(
        functools.partial(
            merge_kernel, n_grp=n_grp, n_seq=n_seq, per_group=blocks // n_grp
        ),
        out_shape=jax.ShapeDtypeStruct((rows * heads, LAT), jnp.bfloat16),
        in_specs=[SMEM] + [VMEM] * (4 + n_grp) + [ANY],
        out_specs=ANY,
        input_output_aliases={5 + n_grp: 0},
        scratch_shapes=[
            pltpu.VMEM((MAXIN * heads, width), jnp.bfloat16),
            pltpu.VMEM((MAXIN * BLOCK, width), jnp.bfloat16),
            pltpu.VMEM((MAXIN * heads, LAT), jnp.bfloat16),
            pltpu.SemaphoreType.DMA((MAXIN,)),
        ],
        compiler_params=pltpu.CompilerParams(vmem_limit_bytes=GRANT),
        name="merge",
    )(table, q_fast, *[fast(x) for x in kept], *landed, out)
    return out.reshape(1, 1, rows, heads, LAT)


def solution(mesh):
    return jax.shard_map(
        local,
        mesh=mesh,
        in_specs=(
            P("side", "grp", "seq", None, None),
            P("side", "grp", "seq", None),
            P("grp", "seq", None),
            P(("grp", "seq"), None),
            P(("grp", "seq"), None),
            P(),
            P(),
        ),
        out_specs=P("side", "grp", "seq", None, None),
        check_vma=False,
    )
```

```python
import functools
import math

import jax
import jax.numpy as jnp
from jax import lax
from jax.experimental import pallas as pl
from jax.experimental.pallas import tpu as pltpu
from jax.sharding import PartitionSpec as P

LAT = 512
ROPE = 64
NOPE = 128
BLOCK = 32
MAXIN = 4
MOSTLEN = 256
SCORES = 2**19
TILE = 256
LANE = 128
AT_ONCE = 4
TOGETHER = 2
SCALE2 = math.log2(math.e) / math.sqrt(NOPE + ROPE)


NT = (((1,), (1,)), ((), ()))
ANY = pl.BlockSpec(memory_space=pl.ANY)
VMEM = pl.BlockSpec(memory_space=pltpu.VMEM)
SMEM = pl.BlockSpec(memory_space=pltpu.SMEM)


GRANT = 40 * 2**20


def far_order(n_seq):
    return [0, 1, *range(n_seq - 1, 1, -1)] if n_seq > 1 else [0]


def fast(x):
    return pltpu.with_memory_space_constraint(x, pltpu.VMEM)


def slow(x):
    return pltpu.with_memory_space_constraint(x, pltpu.HBM)


def fast_shape(shape, dtype):
    return pltpu.VMEM(shape, dtype)


PLACE = 3
RANKS = 2


def fetch_kernel(info_ref, q_hbm, table, q_out, counts, sem, *, blocks, n_grp, n_seq):
    copy = pltpu.make_async_copy(q_hbm, q_out, sem)

    @pl.when(info_ref[0] == 0)
    def _():
        copy.start()

    me = info_ref[1] * n_seq + info_ref[2]
    slots = RANKS + blocks
    table[0] = info_ref[0]
    table[1] = info_ref[1]

    @pl.loop(0, n_grp * n_seq)
    def _(o):
        counts[o] = 0

    for j in range(MAXIN):
        table[slots + 1 + j] = 0
        table[slots + 1 + MAXIN + j] = -1

    @pl.loop(0, blocks)
    def _(b):
        owner = info_ref[PLACE + b]
        rank = counts[owner]
        table[RANKS + b] = rank
        counts[owner] = rank + 1

        @pl.when(owner == me)
        def _():
            table[slots + 1 + rank] = b
            table[slots + 1 + MAXIN + rank] = info_ref[PLACE + blocks + b]

    table[slots] = counts[me]

    @pl.when(info_ref[0] == 0)
    def _():
        copy.wait()


class Slots:
    def __init__(self, table):
        self.table, self.at = table, table.shape[0] - 2 * MAXIN - 1

    def count(self):
        return self.table[self.at]

    def block(self, j):
        return self.table[self.at + 1 + j]

    def request(self, j):
        return self.table[self.at + 1 + MAXIN + j]


def pick_kernel(info, table, *refs, n_seq, n_grp):
    chunks, outs = refs[:n_seq], refs[n_seq:]
    side, grp, seq = info[0], info[1], info[2]
    per_device = chunks[0].shape[0] // 2 // BLOCK

    @pl.when(side == 0)
    def _():
        for i, far in enumerate(far_order(n_seq)):
            for half in range(per_device):
                b = (grp * n_seq + (seq ^ far)) * per_device + half
                owner = info[PLACE + b]
                apart = (owner // n_seq) ^ grp
                at = pl.multiple_of(table[RANKS + b] * BLOCK, BLOCK)

                @pl.when(owner % n_seq == seq)
                def _(i=i, half=half, at=at, apart=apart):
                    for d in range(n_grp):

                        @pl.when(apart == d)
                        def _(d=d):
                            outs[d][pl.ds(at, BLOCK), :] = chunks[i][
                                half * BLOCK : (half + 1) * BLOCK, :
                            ]


def main_kernel(info, table, q_ref, q_hbm, cache_hbm, *refs, n_seq, blocks, step):
    chunks = refs[:n_seq]
    out_hbm, kept_q, kept_acc, kept_max, kept_sum = refs[n_seq : n_seq + 5]
    (kbuf, qbuf, cbuf, obuf, dbuf, scores_ref, best, sums, acc, own32, offsets) = refs[
        n_seq + 5 : -3
    ]
    qsem, csem, osem = refs[-3:]
    side, seq = info[0], info[2]
    requests = chunks[0].shape[0] // 2
    heads = q_ref.shape[0] // requests
    steps = q_ref.shape[0] // step
    per_step = step // heads

    def o_copy(t):
        return pltpu.make_async_copy(
            obuf.at[t % 2], out_hbm.at[t * step : (t + 1) * step, :], osem.at[t % 2]
        )

    def prefill(keys, tail):
        col = lax.broadcasted_iota(jnp.int32, (1, tail), 1)
        least = col - seq * requests

        def score(t):
            scores_ref[:, : keys + tail] = lax.dot_general(
                q_ref[t * step : (t + 1) * step, :],
                kbuf[: keys + tail, :],
                NT,
                preferred_element_type=jnp.float32,
            )

        def finish(t):
            scores = scores_ref[:, : keys + tail]
            late = []
            for k in range(per_step):
                hidden = jnp.where(least <= t * per_step + k, 0.0, -jnp.inf)
                late.append(scores[k * heads : (k + 1) * heads, keys:] + hidden)
            late = jnp.concatenate(late, 0)
            early = scores[:, :keys]
            top = jnp.maximum(
                jnp.max(early, axis=1, keepdims=True), jnp.max(late, axis=1, keepdims=True)
            )
            shift = top * SCALE2
            early = jnp.exp2(early * SCALE2 - shift)
            late = jnp.exp2(late * SCALE2 - shift)
            total = jnp.sum(early, axis=1, keepdims=True) + jnp.sum(late, axis=1, keepdims=True)
            lifted = jnp.concatenate([early.astype(jnp.bfloat16), late.astype(jnp.bfloat16)], 1)
            mixed = jnp.dot(lifted, kbuf[: keys + tail, :LAT], preferred_element_type=jnp.float32)
            if t >= 2:
                o_copy(t - 2).wait()
            obuf[t % 2] = (mixed * (1.0 / total)).astype(jnp.bfloat16)
            o_copy(t).start()

        for t in range(steps):
            score(t)
            finish(t)
        o_copy(steps - 2).wait()
        o_copy(steps - 1).wait()

    @pl.when(side == 0)
    def _():
        half = chunks[0].shape[0] // 2
        keys = n_seq * half
        for i, far in enumerate(far_order(n_seq)):
            kbuf[i * half : (i + 1) * half, :] = chunks[i][:half, :]
            to = pl.multiple_of(keys + (seq ^ far) * half, half)
            kbuf[pl.ds(to, half), :] = chunks[i][half:, :]

        few = keys // 2 if n_seq % 2 == 0 else keys

        @pl.when(seq * half < few)
        def _():
            prefill(keys, few)

        if few < keys:

            @pl.when(seq * half >= few)
            def _():
                prefill(keys, keys)

    @pl.when(side == 1)
    def _():
        chunks_in = cache_hbm.shape[1] // TILE
        lanes = cache_hbm.shape[1] // LANE
        size = AT_ONCE * heads
        bodies = requests // AT_ONCE

        def c_copy(k):
            at = pl.multiple_of(k * TILE, TILE)
            return pltpu.make_async_copy(
                cache_hbm.at[:, pl.ds(at, TILE)], cbuf.at[:, pl.ds(at, TILE)], csem.at[k]
            )

        def d_copy(t):
            at = pl.multiple_of(t * size, size)
            return pltpu.make_async_copy(
                dbuf.at[t % 2], out_hbm.at[pl.ds(at, size), :], osem.at[t % 2]
            )

        def q_copy(t):
            at = pl.multiple_of(t * size, size)
            return pltpu.make_async_copy(
                q_hbm.at[pl.ds(at, size), :], qbuf.at[pl.ds(at, size), :], qsem.at[t]
            )

        @pl.loop(0, max(chunks_in, bodies))
        def _(k):
            @pl.when(k < bodies)
            def _():
                q_copy(k).start()

            @pl.when(k < chunks_in)
            def _():
                c_copy(k).start()

        own32[...] = chunks[0][:requests, :].astype(jnp.float32)
        offsets[0] = 0

        @pl.loop(0, requests)
        def _(r):
            offsets[r + 1] = offsets[r] + info[PLACE + 2 * blocks + r]

        slots = Slots(table)

        def body(t, count):
            span = count * LANE
            lane = lax.broadcasted_iota(jnp.int32, (1, span), 1)
            pairs = range(AT_ONCE // TOGETHER)
            wide = TOGETHER * heads
            first = t * AT_ONCE
            at = pl.multiple_of(first * heads, size)
            low = [offsets[first + u] for u in range(AT_ONCE + 1)]
            start = [
                pl.multiple_of(
                    jnp.minimum(low[p * TOGETHER] // LANE, lanes - count) * LANE, LANE
                )
                for p in pairs
            ]
            q = qbuf[pl.ds(at, size), :]
            q = [q[p * wide : (p + 1) * wide] for p in pairs]
            own = [own32[pl.ds(first + u, 1), :] for u in range(AT_ONCE)]
            scores = [
                jnp.dot(q[p], cbuf[:, pl.ds(start[p], span)], preferred_element_type=jnp.float32)
                for p in pairs
            ]
            itself = []
            for p in pairs:
                alone = [
                    jnp.sum(
                        q[p][k * heads : (k + 1) * heads].astype(jnp.float32)
                        * own[p * TOGETHER + k],
                        axis=1,
                        keepdims=True,
                    )
                    for k in range(TOGETHER)
                ]
                itself.append(jnp.concatenate(alone, 0))
                place = lane + start[p]
                shown = []
                for k in range(TOGETHER):
                    u = p * TOGETHER + k
                    hidden = jnp.where((place >= low[u]) & (place < low[u + 1]), 0.0, -jnp.inf)
                    shown.append(scores[p][k * heads : (k + 1) * heads] + hidden)
                scores[p] = jnp.concatenate(shown, 0)
            top = [
                jnp.maximum(jnp.max(scores[p], axis=1, keepdims=True), itself[p]) for p in pairs
            ]
            lifted = [jnp.exp2(scores[p] * SCALE2 - top[p] * SCALE2) for p in pairs]
            lead = [jnp.exp2((itself[p] - top[p]) * SCALE2) for p in pairs]
            mixed = [
                lax.dot_general(
                    lifted[p].astype(jnp.bfloat16),
                    cbuf[:LAT, pl.ds(start[p], span)],
                    NT,
                    preferred_element_type=jnp.float32,
                )
                for p in pairs
            ]
            total = [lead[p] + jnp.sum(lifted[p], axis=1, keepdims=True) for p in pairs]
            for p in pairs:
                added = [
                    lead[p][k * heads : (k + 1) * heads] * own[p * TOGETHER + k][:, :LAT]
                    for k in range(TOGETHER)
                ]
                mixed[p] = mixed[p] + jnp.concatenate(added, 0)
            scaled = [(mixed[p] * (1.0 / total[p])).astype(jnp.bfloat16) for p in pairs]
            whole = pl.ds(at, size)
            dbuf[t % 2] = jnp.concatenate(scaled, 0)
            acc[whole, :] = jnp.concatenate(mixed, 0)
            best[whole, :] = jnp.broadcast_to(jnp.concatenate(top, 0), (size, LANE))
            sums[whole, :] = jnp.broadcast_to(jnp.concatenate(total, 0), (size, LANE))

        def one_body(t, ready):
            first = t * AT_ONCE

            count = 1
            for u in range(0, AT_ONCE, TOGETHER):
                low, high = offsets[first + u], offsets[first + u + TOGETHER]
                count = jnp.maximum(count, (high + LANE - 1) // LANE - low // LANE)
            last = offsets[first + AT_ONCE - TOGETHER]
            end = jnp.minimum(last // LANE, lanes - count) + count
            need = (end * LANE + TILE - 1) // TILE

            @pl.loop(ready, need)
            def _(k):
                c_copy(k).wait()

            q_copy(t).wait()

            @pl.when(t >= 2)
            def _():
                d_copy(t - 2).wait()

            for c in range(1, TOGETHER * MOSTLEN // LANE + 2):

                @pl.when(count == c)
                def _(c=c):
                    body(t, c)

            d_copy(t).start()
            return jnp.maximum(ready, need)

        ready = lax.fori_loop(0, bodies, one_body, 0)

        @pl.loop(ready, chunks_in)
        def _(k):
            c_copy(k).wait()

        for j in range(MAXIN):
            at = pl.multiple_of(jnp.maximum(slots.request(j), 0) * heads, heads)
            to = slice(j * heads, (j + 1) * heads)
            kept_q[to, :] = qbuf[pl.ds(at, heads), :]
            kept_acc[to, :] = acc[pl.ds(at, heads), :]
            kept_max[to, :] = best[pl.ds(at, heads), :]
            kept_sum[to, :] = sums[pl.ds(at, heads), :]
        d_copy(bodies - 2).wait()
        d_copy(bodies - 1).wait()


def merge_kernel(
    table,
    kept_q,
    kept_acc,
    kept_max,
    kept_sum,
    *refs,
    n_grp,
    n_seq,
    per_group,
):
    landed, out_hbm = refs[:n_grp], refs[n_grp + 1]
    arrived, obuf, osem = refs[n_grp + 2 :]
    side, grp = table[0], table[1]
    heads = kept_q.shape[0] // MAXIN
    slots = Slots(table)

    @pl.when((side == 1) & (slots.count() > 0))
    def _():
        arrived[...] = jnp.zeros_like(arrived)

        def o_copy(j):
            at = pl.multiple_of(jnp.maximum(slots.request(j), 0) * heads, heads)
            return pltpu.make_async_copy(
                obuf.at[j * heads : (j + 1) * heads, :],
                out_hbm.at[pl.ds(at, heads), :],
                osem.at[j],
            )

        def written(j):
            wanted = j < slots.count()
            for k in range(j):
                wanted = wanted & (slots.request(k) != slots.request(j))
            return wanted

        for j in range(MAXIN):
            apart = (slots.block(j) // per_group) ^ grp
            for d in range(n_grp):

                @pl.when((j < slots.count()) & (apart == d))
                def _(j=j, d=d):
                    rows = slice(j * BLOCK, (j + 1) * BLOCK)
                    arrived[rows, :] = landed[d][rows, :]

        def spread(index, size):
            value = slots.request(MAXIN - 1)
            for j in range(MAXIN - 2, -1, -1):
                value = jnp.where(index < (j + 1) * size, slots.request(j), value)
            return value

        query = lax.broadcasted_iota(jnp.int32, (MAXIN * heads, 1), 0)
        key = lax.broadcasted_iota(jnp.int32, (1, MAXIN * BLOCK), 1)
        allowed = (spread(query, heads) == spread(key, BLOCK)) & (key < slots.count() * BLOCK)
        live = query < slots.count() * heads
        scores = lax.dot_general(kept_q[...], arrived[...], NT, preferred_element_type=jnp.float32)
        top = jnp.where(live, kept_max[:, :1], 0.0)
        scores = jnp.where(allowed, scores, -jnp.inf)
        higher = jnp.maximum(top, jnp.max(scores, axis=1, keepdims=True))
        shift = higher * SCALE2
        lifted = jnp.exp2(scores * SCALE2 - shift)
        fade = jnp.exp2(top * SCALE2 - shift)
        total = kept_sum[:, :1] * fade + jnp.sum(lifted, axis=1, keepdims=True)
        mixed = kept_acc[...] * fade + jnp.dot(
            lifted.astype(jnp.bfloat16), arrived[:, :LAT], preferred_element_type=jnp.float32
        )
        obuf[...] = (mixed * (1.0 / total)).astype(jnp.bfloat16)
        for j in range(MAXIN):

            @pl.when(written(j))
            def _(j=j):
                o_copy(j).start()

        for j in range(MAXIN):

            @pl.when(written(j))
            def _(j=j):
                o_copy(j).wait()


def local(
    queries, stream_rows, span_latents, decode_cache, cache_lengths, block_owner, block_request
):
    n_grp, n_side, n_seq = (lax.axis_size(a) for a in ("grp", "side", "seq"))
    names = ("grp", "side", "seq")
    place = [lax.axis_index(a).astype(jnp.int32).reshape(1) for a in ("side", "grp", "seq")]
    blocks = block_request.shape[0]
    info = jnp.concatenate([*place, block_owner[:, 0], block_request, cache_lengths[0]])
    own_query, own_stream, own_span = queries[0, 0], stream_rows[0, 0], span_latents[0]
    rows, heads, width = own_query.shape
    q = slow(own_query.reshape(rows * heads, width))
    size = RANKS + blocks + 1 + 2 * MAXIN
    cache = slow(decode_cache.T)

    def at(grp, side, seq):
        return (grp * n_side + side) * n_seq + seq

    def along_seq(far):
        return [
            (at(g, 0, s), at(g, 0, s ^ far)) for g in range(n_grp) for s in range(n_seq)
        ]

    def across(apart):
        return [
            (at(g, 0, s), at(g ^ apart, 1, s)) for g in range(n_grp) for s in range(n_seq)
        ]

    chunk = jnp.concatenate([own_stream, own_span], 0)
    chunks = [fast(chunk)]
    for far in far_order(n_seq)[1:]:
        chunks.append(fast(lax.ppermute(chunk, names, along_seq(far))))

    table, q_fast = pl.pallas_call(
        functools.partial(fetch_kernel, blocks=blocks, n_grp=n_grp, n_seq=n_seq),
        out_shape=[jax.ShapeDtypeStruct((size,), jnp.int32), fast_shape(q.shape, q.dtype)],
        in_specs=[SMEM, ANY],
        out_specs=[SMEM, VMEM],
        scratch_shapes=[pltpu.SMEM((n_grp * n_seq,), jnp.int32), pltpu.SemaphoreType.DMA],
        compiler_params=pltpu.CompilerParams(vmem_limit_bytes=GRANT),
        cost_estimate=pl.CostEstimate(flops=0, bytes_accessed=4 * q.size, transcendentals=0),
        name="fetch",
    )(info, q)
    q_fast = fast(q_fast)

    picked = pl.pallas_call(
        functools.partial(pick_kernel, n_seq=n_seq, n_grp=n_grp),
        out_shape=[fast_shape((MAXIN * BLOCK, width), jnp.bfloat16)] * n_grp,
        in_specs=[SMEM, SMEM] + [VMEM] * n_seq,
        out_specs=[VMEM] * n_grp,
        compiler_params=pltpu.CompilerParams(vmem_limit_bytes=GRANT),
        name="pick",
    )(info, table, *chunks)
    landed = [fast(lax.ppermute(picked[d], names, across(d))) for d in range(n_grp)]

    tiles = cache.shape[1] // TILE
    keys = n_seq * 2 * rows
    step = min(rows * heads, max(heads, SCORES // keys))
    stats = fast_shape((MAXIN * heads, 128), jnp.float32)
    out, *kept = pl.pallas_call(
        functools.partial(main_kernel, n_seq=n_seq, blocks=blocks, step=step),
        out_shape=[
            jax.ShapeDtypeStruct((rows * heads, LAT), jnp.bfloat16),
            fast_shape((MAXIN * heads, width), jnp.bfloat16),
            fast_shape((MAXIN * heads, LAT), jnp.float32),
            stats,
            stats,
        ],
        in_specs=[SMEM, SMEM, VMEM, ANY, ANY] + [VMEM] * n_seq,
        out_specs=[ANY] + [VMEM] * 4,
        scratch_shapes=[
            pltpu.VMEM((keys, width), jnp.bfloat16),
            pltpu.VMEM(q.shape, jnp.bfloat16),
            pltpu.VMEM(cache.shape, jnp.bfloat16),
            pltpu.VMEM((2, step, LAT), jnp.bfloat16),
            pltpu.VMEM((2, AT_ONCE * heads, LAT), jnp.bfloat16),
            pltpu.VMEM((step, keys), jnp.float32),
            pltpu.VMEM((rows * heads, LANE), jnp.float32),
            pltpu.VMEM((rows * heads, LANE), jnp.float32),
            pltpu.VMEM((rows * heads, LAT), jnp.float32),
            pltpu.VMEM((rows, width), jnp.float32),
            pltpu.SMEM((rows + 1,), jnp.int32),
            pltpu.SemaphoreType.DMA((rows // AT_ONCE,)),
            pltpu.SemaphoreType.DMA((tiles,)),
            pltpu.SemaphoreType.DMA((2,)),
        ],
        compiler_params=pltpu.CompilerParams(vmem_limit_bytes=GRANT),
        cost_estimate=pl.CostEstimate(
            flops=2 * rows * heads * keys * (width + LAT),
            bytes_accessed=2 * (q.size + cache.size + rows * heads * LAT),
            transcendentals=rows * heads * keys,
        ),
        name="main",
    )(info, table, q_fast, q, cache, *chunks)

    out = pl.pallas_call(
        functools.partial(
            merge_kernel, n_grp=n_grp, n_seq=n_seq, per_group=blocks // n_grp
        ),
        out_shape=jax.ShapeDtypeStruct((rows * heads, LAT), jnp.bfloat16),
        in_specs=[SMEM] + [VMEM] * (4 + n_grp) + [ANY],
        out_specs=ANY,
        input_output_aliases={5 + n_grp: 0},
        scratch_shapes=[
            pltpu.VMEM((MAXIN * BLOCK, width), jnp.bfloat16),
            pltpu.VMEM((MAXIN * heads, LAT), jnp.bfloat16),
            pltpu.SemaphoreType.DMA((MAXIN,)),
        ],
        compiler_params=pltpu.CompilerParams(vmem_limit_bytes=GRANT),
        name="merge",
    )(table, *[fast(x) for x in kept], *landed, out)
    return out.reshape(1, 1, rows, heads, LAT)


def solution(mesh):
    return jax.shard_map(
        local,
        mesh=mesh,
        in_specs=(
            P("side", "grp", "seq", None, None),
            P("side", "grp", "seq", None),
            P("grp", "seq", None),
            P(("grp", "seq"), None),
            P(("grp", "seq"), None),
            P(),
            P(),
        ),
        out_specs=P("side", "grp", "seq", None, None),
        check_vma=False,
    )
```
